128 devices in a mesh: front: 8 (over x, core), grp: 16 (over y, z).
Axes of the slice: x: 4, y: 4, z: 4, core: 2. Of those that a mesh axis runs over, the one named last changes fastest.
Arguments:
- contributions: bfloat16 [16384, 16384], P(('front', 'grp')), may hold values from -6 to 6
- sketch_matrix: bfloat16 [16384, 256], P(('front', 'grp')), may hold values from -0.046875 to 0.046875
- destinations: int32 [16384, 1], replicated, may hold values from 0 to 127; in each aligned block of 128 rows (0 to 127, 128 to 255, ...) at most 2 rows name the same one
- parent_rows: int32 [16384], replicated, may hold values from 0 to 1023
- front_sizes: int32 [8], P('front'), may hold values from 8192 to 16384
- leaf_skeleton: int32 [8, 16, 128], P('front', 'grp'), may hold values from 0 to 1023, as said below
- merge_skeleton: int32 [8, 14, 128], P('front'), may hold values from 0 to 255, as said below
Outputs:
- leaf_maps: float32 [8, 16384, 128], P('front', 'grp')
- node_maps: float32 [8, 16, 3, 256, 128], P('front', 'grp')
- top_rows: float32 [8, 16, 128, 256], P('front', 'grp')
The draws below stay inside these ranges and needn't reach their ends.
Inputs may be any that keep to these rules, and one draw needn't show every extreme that they name: `destinations`: in the rows of one device no destination is named by more than 2 rows. `leaf_skeleton`: each row holds 128 different row numbers of a leaf block. `merge_skeleton`: each row holds 128 different positions of the stacked 2 * 128 rows.
All inputs are finite; a program needn't handle non-finite values.
Results may differ from the reference program's by a relative error of at most 0.003.
Values may be sent and summed in bfloat16 or wider, within the bound.
No kernel may reach another device: no remote copies, remote signals or barrier semaphores. Data moves between devices by JAX's collectives and lax.ppermute only.
A program may use at most 64 MiB of HBM per device.

```python
import math
import jax
import jax.numpy as jnp
import numpy as np
from jax import lax

CHILD_ORDER = 16384
SKETCH = 256
K = 128
PR_DEV = 1024
LEVELS = 3
CHILD_DEV = 128
FRONTS = 8
LEAVES = 16
PROWS = 16384
NODES = 14
CAP = 2
DEVICES = 128


def distinct_rows(key, count, length, keep):
    scores = jax.random.randint(key, (count, length), 0, 2 ** 20) * length + jnp.arange(length, dtype=jnp.int32)[None, :]
    order = jnp.argsort(scores, axis=-1, stable=True)
    return order[:, :keep].astype(jnp.int32)


def draw_leaf_skeleton(key, part):
    picked = distinct_rows(jax.random.fold_in(key, 11), FRONTS * LEAVES, PR_DEV, K)
    return picked.reshape(FRONTS, LEAVES, K)


def draw_merge_skeleton(key, part):
    picked = distinct_rows(jax.random.fold_in(key, 23), FRONTS * NODES, 2 * K, K)
    return picked.reshape(FRONTS, NODES, K)


def place_ends(array, key, low, high):
    dims = array.shape
    index_at = [jax.random.randint(jax.random.fold_in(key, axis), (), 0, dims[axis]) for axis in range(len(dims))]
    array = array.at[tuple(index_at)].set(low)
    longest = dims.index(max(dims))
    index_at[longest] = (index_at[longest] + 1) % dims[longest]
    return array.at[tuple(index_at)].set(high)


def block_levels(rng, extent, split, smallest, largest):
    gain = 1.0
    for axis_at, parts in split:
        steps = jax.random.uniform(jax.random.fold_in(jax.random.fold_in(rng, 6), axis_at), (parts,), jnp.float32, smallest / len(split), largest / len(split))
        gain = gain * jnp.repeat(jnp.exp(steps), extent[axis_at] // parts).reshape((-1,) + (1,) * (len(extent) - 1 - axis_at))
    return gain


def assign_block(rng, own, number, rows, amount, top, bound, skew):
    order = jax.random.permutation(rng, amount)
    heavy_load, common = shares(amount, rows * top, bound, skew, True), shares(amount, rows * top, bound, skew, False)
    places = jnp.arange(amount)

    def named(sizes, offset_by):
        used = int((sizes > 0).sum())
        fixed = max(1, used // 4)
        shifted = fixed + (places - fixed + offset_by * (used - fixed)) % max(1, amount - fixed)
        return jnp.zeros((amount,), jnp.int32).at[order[jnp.where(places < fixed, places, shifted)]].set(jnp.asarray(sizes, jnp.int32))

    sizes = jnp.where(number % 4 == 0, named(heavy_load, number // 4), named(common, number - number // 4 - 1))
    mixed = jax.random.permutation(jax.random.fold_in(own, 3), amount)
    giver, receiver = mixed[0:amount // 2 * 2:2], mixed[1:amount // 2 * 2:2]
    room = jnp.minimum(sizes[giver] - 1, bound - sizes[receiver]) // 2
    room = jnp.where((giver == order[0]) | (receiver == order[0]) | (sizes[receiver] == 0), 0, jnp.maximum(room, 0))
    shifted = jax.random.randint(jax.random.fold_in(own, 4), (amount // 2,), 0, 1 << 20) % (room + 1)
    sizes = sizes.at[giver].add(-shifted).at[receiver].add(shifted)
    labels = jnp.searchsorted(jnp.cumsum(sizes), jnp.arange(rows * top), side="right").astype(jnp.int32)
    table = labels.reshape(top, rows).T
    table = table[jax.random.permutation(jax.random.fold_in(own, 1), rows)]
    offset_by = jax.random.randint(jax.random.fold_in(own, 2), (rows, 1), 0, top)
    return jnp.take_along_axis(table, (jnp.arange(top)[None, :] + offset_by) % top, axis=1)


def shares(count, total, limit, skew, full):
    weights = [(1 << 20) // math.isqrt(standing ** skew) + 1 for standing in range(1, count + 1)]
    largest = limit if full else min(limit, max(-(-total // count), total * weights[0] // sum(weights)))
    least = 1 if total - largest >= count - 1 else 0
    holding, rest = [largest] + [least] * (count - 1), total - largest - least * (count - 1)
    while rest > 0:
        free = [i for i in range(1, count) if holding[i] < largest] or [i for i in range(1, count) if holding[i] < limit]
        whole, left = sum([weights[i] for i in free]), rest
        for i in free:
            more = min(limit - holding[i], max(1, left * weights[i] // whole), rest)
            holding[i] = holding[i] + more
            rest = rest - more
    return np.array(holding)


def noise(stream_key, shape, deviation, reach, pieces=(), kind=jnp.bfloat16):
    array = deviation * jax.random.normal(stream_key, shape, jnp.float32)
    if pieces:
        array = array * block_levels(stream_key, shape, pieces, -0.22, 0.18)
    return jnp.clip(array, -reach, reach).astype(kind)


def setup_inputs(seed: int = 0) -> dict:
    splits = jax.random.split(jax.random.key(seed), 8)
    contributions = noise(splits[0], (DEVICES * CHILD_DEV, CHILD_ORDER), 1.0, 6.0, ((0, 128),))
    sketch_matrix = noise(splits[1], (CHILD_ORDER, SKETCH), CHILD_ORDER ** -0.5, 0.046875, ((0, 128),))
    destinations_keys = jax.random.split(jax.random.fold_in(splits[2], 1), (DEVICES * CHILD_DEV) // CHILD_DEV)
    destinations_turns = jax.random.permutation(jax.random.fold_in(splits[2], 3), (DEVICES * CHILD_DEV) // CHILD_DEV)
    destinations = jax.vmap(lambda own, number: assign_block(jax.random.fold_in(splits[2], 2), own, number, CHILD_DEV, DEVICES, 1, CAP, 1))(destinations_keys, destinations_turns).reshape((DEVICES * CHILD_DEV, 1))
    parent_rows = place_ends(jax.random.randint(splits[3], (DEVICES * CHILD_DEV,), 0, PR_DEV), jax.random.fold_in(splits[3], 1), 0, PR_DEV - 1).astype(jnp.int32)
    front_sizes = place_ends(jax.random.randint(splits[4], (FRONTS,), PROWS // 2, PROWS + 1), jax.random.fold_in(splits[4], 1), PROWS // 2, PROWS).astype(jnp.int32)
    leaf_skeleton = draw_leaf_skeleton(jax.random.fold_in(splits[7], 71), 0)
    merge_skeleton = draw_merge_skeleton(jax.random.fold_in(splits[7], 71), 0)
    return {"contributions": contributions, "sketch_matrix": sketch_matrix, "destinations": destinations, "parent_rows": parent_rows, "front_sizes": front_sizes, "leaf_skeleton": leaf_skeleton, "merge_skeleton": merge_skeleton}


def ridge_map(rows, basis):
    gram = jnp.dot(basis, basis.T, precision=lax.Precision.HIGHEST)
    shift = 0.1 * jnp.mean(jnp.diagonal(gram)) + 1e-5
    ident = jnp.eye(gram.shape[0], dtype=jnp.float32)
    gram = gram + shift * ident
    approx = ident / jnp.trace(gram)
    for step in range(24):
        approx = jnp.dot(approx, 2.0 * ident - jnp.dot(gram, approx, precision=lax.Precision.HIGHEST), precision=lax.Precision.HIGHEST)
    right = jnp.dot(rows, basis.T, precision=lax.Precision.HIGHEST)
    return jnp.dot(right, approx, precision=lax.Precision.HIGHEST)


def reference(contributions, sketch_matrix, destinations, parent_rows, front_sizes, leaf_skeleton, merge_skeleton):
    blocks = contributions.reshape(DEVICES, CHILD_DEV, CHILD_ORDER)
    sketch = lax.map(lambda block: jnp.dot(block, sketch_matrix, preferred_element_type=jnp.float32).astype(jnp.bfloat16), blocks)
    sketch = sketch.reshape(DEVICES * CHILD_DEV, SKETCH).astype(jnp.float32)
    target = destinations[:, 0] * PR_DEV + parent_rows
    parent = jax.ops.segment_sum(sketch, target, num_segments=DEVICES * PR_DEV).reshape(FRONTS, PROWS, SKETCH)
    keep = jnp.arange(PROWS, dtype=jnp.int32)[None, :] < front_sizes[:, None]
    parent = jnp.where(keep[:, :, None], parent, jnp.zeros_like(parent))
    blocks_y = parent.reshape(FRONTS, LEAVES, PR_DEV, SKETCH)
    pick = jax.vmap(jax.vmap(lambda rows, index: jnp.take(rows, index, axis=0)))
    solve = jax.vmap(jax.vmap(ridge_map))
    bases = pick(blocks_y, leaf_skeleton)
    leaf_maps = solve(blocks_y, bases).reshape(FRONTS, PROWS, K)
    count = LEAVES
    level_maps = []
    for level in range(LEVELS):
        offset = LEAVES - count
        stacked = bases.reshape(FRONTS, count // 2, 2 * K, SKETCH)
        chosen = merge_skeleton[:, offset:offset + count // 2]
        bases = pick(stacked, chosen)
        maps = solve(stacked, bases)
        level_maps.append(jnp.repeat(maps, 2 ** (level + 1), axis=1))
        count = count // 2
    node_maps = jnp.stack(level_maps, axis=2)
    top_rows = jnp.repeat(bases, 2 ** LEVELS, axis=1)
    return leaf_maps, node_maps, top_rows
```

```python
import functools

import jax
import jax.numpy as jnp
from jax import lax
from jax.experimental import pallas as pl
from jax.experimental.pallas import tpu as pltpu
from jax.sharding import Mesh
from jax.sharding import PartitionSpec as P

PR_DEV = 1024
LEVELS = 3
ROWS = 128
WIDTH = 256
HALF = 128
K = 128
DOUBLINGS = 8
ALL = ("x", "core", "grp")
F32 = jnp.float32
BF16 = jnp.bfloat16
HIGH = lax.Precision.HIGHEST


def coords(device):
    front, grp = device // 16, device % 16
    return [front >> 1, grp >> 2, grp & 3], front & 1


def device_of(chip, core):
    return (chip[0] * 2 + core) * 16 + chip[1] * 4 + chip[2]


def route(axis, masks):
    pairs = []
    for device in range(128):
        chip, core = coords(device)
        chip[axis] ^= masks[core]
        pairs.append((device, device_of(chip, core)))
    return pairs


def core_route():
    pairs = []
    for device in range(128):
        chip, core = coords(device)
        pairs.append((device, device_of(chip, 1 - core)))
    return pairs


def send(value, pairs):
    return lax.ppermute(value, ALL, pairs)


def vmem():
    return pl.BlockSpec(memory_space=pltpu.VMEM)


def smem():
    return pl.BlockSpec(memory_space=pltpu.SMEM)


def hbm():
    return pl.BlockSpec(memory_space=pl.ANY)


def call(kernel, outs, args, specs, out_specs, scratch=(), name=None, flops=0, aliases=None, limit=6):
    return pl.pallas_call(
        kernel,
        out_shape=outs,
        in_specs=specs,
        out_specs=out_specs,
        scratch_shapes=list(scratch),
        input_output_aliases=aliases or {},
        cost_estimate=pl.CostEstimate(flops=flops, bytes_accessed=1 << 20, transcendentals=0),
        compiler_params=pltpu.CompilerParams(vmem_limit_bytes=limit << 20),
        name=name,
    )(*args)


def split3(value):
    hi = value.astype(BF16)
    rest = value - hi.astype(F32)
    mid = rest.astype(BF16)
    low = (rest - mid.astype(F32)).astype(BF16)
    return hi, mid, low


def pick(onehot, value):
    out = None
    for term in split3(value):
        part = jnp.dot(onehot, term, preferred_element_type=F32)
        out = part if out is None else out + part
    return out


def extract_kernel(where, full, out):
    out[...] = full[...]


def other_half(contributions, core):
    return pl.pallas_call(
        extract_kernel,
        out_shape=jax.ShapeDtypeStruct((ROWS, 8192), BF16),
        grid_spec=pltpu.PrefetchScalarGridSpec(
            num_scalar_prefetch=1,
            grid=(4,),
            in_specs=[pl.BlockSpec((ROWS, 2048), lambda i, s: (0, 2 * i + 1 - s[0]))],
            out_specs=pl.BlockSpec((ROWS, 2048), lambda i, s: (0, i)),
        ),
        compiler_params=pltpu.CompilerParams(vmem_limit_bytes=4 << 20),
        name="other_half",
    )(core.reshape(1), contributions)


def piece_offset(where, order, piece):
    core = where[3]
    first, second = jnp.where(core == 0, 1, 3), jnp.where(core == 0, 3, 1)
    chip = [where[0], where[1], where[2]]
    for step, axis in enumerate(order):
        if (piece >> (2 * step)) & 1:
            chip[axis] = chip[axis] ^ first
        if (piece >> (2 * step + 1)) & 1:
            chip[axis] = chip[axis] ^ second
    inside = chip[1] * 4 + chip[2]
    whole = ((chip[0] * 2 + core) * 16 + inside) * 128
    half = (chip[0] * 16 + inside) * 128
    return pl.multiple_of(whole, 128), pl.multiple_of(half, 128)


ORDERS = ((0, 1, 2), (1, 2, 0))


def partial_products(where, own, received, pieces, first):
    columns = []
    for order, piece in zip(ORDERS, pieces):
        total = [None, None]
        for j in range(0, 32, 2):
            spot = [piece_offset(where, order, first + j), piece_offset(where, order, first + j + 1)]
            right = piece[j : j + 2].reshape(256, HALF)
            for side, source in enumerate((own, received)):
                left = jnp.concatenate([source[:, pl.ds(s[side], 128)] for s in spot], axis=1)
                part = jnp.dot(left, right, preferred_element_type=F32)
                total[side] = part if total[side] is None else total[side] + part
        columns.append(jnp.concatenate(total, axis=0))
    return jnp.concatenate(columns, axis=1)


def first_kernel(where, full, received, a, b, out):
    out[...] = partial_products(where, full, received, (a, b), 0)


def second_kernel(where, keys, full, received, a, b, acc, keep, give):
    total = acc[...] + partial_products(where, full, received, (a, b), 32)
    core = where[3]
    spots = lax.broadcasted_iota(jnp.int32, (256, 256), 0)
    key = keys[...]
    here = (key == spots + core * 256).astype(F32).astype(BF16)
    there = (key == spots + (1 - core) * 256).astype(F32).astype(BF16)
    keep[...] = pick(here, total)
    give[...] = pick(there, total)


def finish_kernel(keep, given, out):
    rows = (keep[...] + given[...]).astype(BF16).reshape(16, 16, WIDTH)
    for copy in range(4):
        out[:, copy] = rows


def join_kernel(a, b, out):
    count = a.shape[0]
    out[:count] = a[...]
    out[count:] = b[...]


def matches(column, row):
    return (column == row).astype(F32).astype(BF16)


def basis_kernel(arrived, landing, keys, out):
    out[...] = jnp.dot(
        matches(keys[...], landing[...]), arrived[...], preferred_element_type=F32
    )


def split2(value):
    hi = value.astype(BF16)
    return hi, (value - hi.astype(F32)).astype(BF16)


def mul(a, b):
    (ah, al), (bh, bl) = split2(a), split2(b)
    wide = jnp.dot(
        jnp.concatenate([ah, al], axis=1),
        jnp.concatenate([bh, bh], axis=0),
        preferred_element_type=F32,
    )
    return wide + jnp.dot(ah, bl, preferred_element_type=F32)


def mul_t(a, b, precision=None):
    dims = (((1,), (1,)), ((), ()))
    if precision is not None:
        return lax.dot_general(a, b, dims, precision=precision, preferred_element_type=F32)
    (ah, al), (bh, bl) = split2(a), split2(b)
    out = None
    for p, q in ((ah, bh), (ah, bl), (al, bh)):
        part = lax.dot_general(p, q, dims, preferred_element_type=F32)
        out = part if out is None else out + part
    return out


def inverses(bases):
    row = lax.broadcasted_iota(jnp.int32, (K, K), 0)
    col = lax.broadcasted_iota(jnp.int32, (K, K), 1)
    ident = (row == col).astype(F32)
    grams = [mul_t(s, s, HIGH) for s in bases]
    state = []
    for index, gram in enumerate(grams):
        trace = jnp.sum(jnp.sum(gram * ident, axis=0, keepdims=True), axis=1, keepdims=True)
        widest = jnp.max(jnp.sum(jnp.abs(gram), axis=0, keepdims=True), axis=1, keepdims=True)
        low = trace * (0.1 / K) + 1e-5
        gram = gram + low * ident
        grams[index] = gram
        high = jnp.maximum(low + jnp.minimum(trace, widest), 2.0 * low)
        scale = 2.0 / (low + high)
        ratio = (high - low) / (high + low)
        residual = ident - scale * gram
        state.append((scale, ratio, residual))
    for index, (scale, ratio, residual) in enumerate(state):
        square = ratio * ratio
        ratio = square / (2.0 - square)
        approx = ((1.0 + ratio) * scale) * (ident + residual)
        residual = (1.0 + ratio) * mul(residual, residual) - ratio * ident
        state[index] = (approx, ratio, residual)
    for step in range(1, DOUBLINGS):
        for index, (approx, ratio, residual) in enumerate(state):
            square = ratio * ratio
            ratio = square / (2.0 - square)
            if step + 1 < DOUBLINGS:
                both = mul(jnp.concatenate([approx, residual], axis=0), residual)
                approx = (1.0 + ratio) * (approx + both[:K])
                residual = (1.0 + ratio) * both[K:] - ratio * ident
            else:
                approx = (1.0 + ratio) * (approx + mul(approx, residual))
            state[index] = (approx, ratio, residual)
    results = []
    for gram, (approx, ratio, residual) in zip(grams, state):
        fix = ident - jnp.dot(gram, approx, precision=HIGH, preferred_element_type=F32)
        results.append((approx, fix))
    return results


def times_inverse(right, approx, fix):
    first = mul(right, approx)
    return first + mul(first, fix)


def choose(flag, first, second):
    return jnp.where(flag == 1, second, first)


def lower_kernel(flags, arrived, landing, own_landing, keys, top, leaf_out, out, built, sem):
    rows = arrived[...]
    stacks = jnp.dot(matches(keys[...], landing[...]), rows, preferred_element_type=F32)
    first, second = stacks[: 2 * K], stacks[2 * K :]
    leaf = choose(flags[0], first[:K], first[K:])
    node = choose(flags[1], second[:K], second[K:])
    bases = [leaf, node, top[...]]
    row = lax.broadcasted_iota(jnp.int32, (256, 1024), 0)
    col = lax.broadcasted_iota(jnp.int32, (256, 1024), 1)
    spot = (row >> 2) * 16 + flags[3] * 4 + (row & 3)
    mine = jnp.dot(matches(spot, col), rows, preferred_element_type=F32)
    rights = [mul_t(v, s) for v, s in zip((mine, first, second), bases)]
    maps = [times_inverse(r, *pair) for r, pair in zip(rights, inverses(bases))]
    for level in range(2):
        built[level] = maps[level + 1]
    copy = pltpu.make_async_copy(built, out.at[:2], sem)
    copy.start()
    spots = lax.broadcasted_iota(jnp.int32, (PR_DEV, 256), 0)
    leaf_out[0] = pick(matches(spots, own_landing[...]), maps[0])
    copy.wait()


def upper_kernel(flags, chosen, current, partner, previous, out, top, built, sem):
    mine, other = current[...], partner[...]
    stacked = jnp.concatenate(
        [choose(flags[2], mine, other), choose(flags[2], other, mine)], axis=0
    )
    spots = lax.broadcasted_iota(jnp.int32, (K, 2 * K), 1)
    basis = pick(matches(chosen[...], spots), stacked)
    top[...] = basis
    right = mul_t(stacked, basis)
    built[...] = times_inverse(right, *inverses([basis])[0])
    copy = pltpu.make_async_copy(built, out.at[2], sem)
    copy.start()
    copy.wait()


def join(a, b, limit):
    return call(
        join_kernel,
        jax.ShapeDtypeStruct((2 * a.shape[0],) + a.shape[1:], a.dtype),
        (a, b),
        [vmem(), vmem()],
        vmem(),
        name="join",
        limit=limit,
    )


def local(contributions, sketch_matrix, destinations, parent_rows, front_sizes, leaf_skeleton, merge_skeleton):
    x, core, grp = lax.axis_index("x"), lax.axis_index("core"), lax.axis_index("grp")
    y, z = grp >> 2, grp & 3
    myself = (x * 2 + core) * 16 + grp
    where = jnp.stack([x, y, z, core]).astype(jnp.int32)

    held = [sketch_matrix[None, :, :HALF], sketch_matrix[None, :, HALF:]]
    side = core
    for step in range(3):
        for half in range(2):
            masks = (1, 3) if half == 0 else (3, 1)
            arriving = [send(held[c], route(ORDERS[c][step], masks)) for c in range(2)]
            if step == 2 and half == 1:
                extra = arriving
            else:
                held = [join(h, r, 4) for h, r in zip(held, arriving)]
            if step == 1 and half == 1:
                (
                    held,
                    side,
                    destinations,
                    parent_rows,
                    front_sizes,
                    leaf_skeleton,
                    merge_skeleton,
                ) = lax.optimization_barrier(
                    (
                        held,
                        core,
                        destinations,
                        parent_rows,
                        front_sizes,
                        leaf_skeleton,
                        merge_skeleton,
                    )
                )
    received = send(other_half(contributions, side), core_route())

    every_dest = destinations[:, 0].reshape(128, ROWS)
    every_row = parent_rows.reshape(128, ROWS)
    later = jnp.arange(ROWS)[:, None] < jnp.arange(ROWS)[None, :]

    def keys_of(device, source_core):
        dest = lax.dynamic_index_in_dim(every_dest, device, 0, keepdims=False)
        same = (dest[:, None] == dest[None, :]) & later
        rank = jnp.sum(same.astype(jnp.int32), axis=0)
        chip = (dest >> 5) * 16 + (dest & 15)
        return ((dest >> 4) & 1) * 256 + chip * 4 + source_core * 2 + rank

    keys = jnp.concatenate(
        [keys_of(myself, core), keys_of((x * 2 + 1 - core) * 16 + grp, 1 - core)]
    ).reshape(1, 256)
    leaves = jnp.arange(4, dtype=jnp.int32)[:, None, None]
    mine = every_dest[None] == leaves + (myself - z)
    before = jnp.dot(
        mine.reshape(512, ROWS).astype(BF16), later.astype(BF16), preferred_element_type=F32
    ).reshape(4, 128, ROWS)
    spots = [
        jnp.sum(jnp.where(mine & (before == slot), every_row[None] + 1, 0), axis=2) - 1
        for slot in range(2)
    ]
    landing = jnp.stack(spots, axis=2)
    live = front_sizes[0] - (y * 4 + leaves) * PR_DEV
    landing = jnp.where((landing >= 0) & (landing < live), landing + leaves * PR_DEV, -1)
    landing = landing.reshape(4, 4, 2, 16, 2).transpose(1, 3, 0, 2, 4)
    own_landing = lax.dynamic_index_in_dim(landing, z, 2, keepdims=False).reshape(1, 256)
    own_landing = jnp.where(own_landing >= 0, own_landing - z * PR_DEV, -1)
    landing = landing.reshape(1, 1024)

    flags = jnp.stack([z & 1, (z >> 1) & 1, y & 1, z]).astype(jnp.int32)
    near = leaf_skeleton.reshape(K) + z * PR_DEV
    side_keys = send(near, route(2, (1, 1)))
    pair = jnp.where(z & 1 == 1, jnp.stack([side_keys, near]), jnp.stack([near, side_keys]))
    pair = pair.reshape(2 * K)
    far = send(pair, route(2, (3, 3)))
    far = far.reshape(2 * K)

    def chosen_of(node):
        return lax.dynamic_index_in_dim(merge_skeleton[0], node, 0, keepdims=False)

    def taken(values, index):
        hit = index[:, None] == jnp.arange(2 * K, dtype=jnp.int32)[None, :]
        return jnp.sum(jnp.where(hit, values[None, :], 0), axis=1)

    low = taken(pair, chosen_of(grp >> 1))
    high = taken(far, chosen_of((grp >> 1) ^ 1))
    swap = (z >> 1) & 1 == 1
    middle = jnp.where(swap, jnp.stack([high, low]), jnp.stack([low, high])).reshape(2 * K)
    top_keys = taken(middle, chosen_of(8 + (grp >> 2))).reshape(K, 1)
    stack_keys = jnp.concatenate([pair, middle]).reshape(4 * K, 1)
    chosen = chosen_of(12 + (grp >> 3)).reshape(K, 1)

    held, keys, landing, own_landing, stack_keys, top_keys, chosen, flags = lax.optimization_barrier(
        (held, keys, landing, own_landing, stack_keys, top_keys, chosen, flags)
    )
    square = jax.ShapeDtypeStruct((256, 256), F32)
    acc = call(
        first_kernel,
        square,
        (where, contributions, received, held[0], held[1]),
        [smem()] + [vmem()] * 4,
        vmem(),
        name="sketch_first",
        flops=1 << 29,
        limit=12,
    )
    keep, give = call(
        second_kernel,
        (square, square),
        (where, keys, contributions, received, extra[0], extra[1], acc),
        [smem()] + [vmem()] * 6,
        (vmem(), vmem()),
        name="sketch_second",
        flops=1 << 29,
        limit=12,
    )
    packed = call(
        finish_kernel,
        jax.ShapeDtypeStruct((16, 4, 16, WIDTH), BF16),
        (keep, send(give, core_route())),
        [vmem(), vmem()],
        vmem(),
        name="finish",
    )
    arrived = lax.all_to_all(
        packed.reshape(64, 16, WIDTH), ("x", "grp"), split_axis=0, concat_axis=0, tiled=True
    ).reshape(1024, WIDTH)

    rows = jax.ShapeDtypeStruct((K, WIDTH), F32)
    current = call(
        basis_kernel, rows, (arrived, landing, top_keys), [vmem()] * 3, vmem(), name="basis", flops=1 << 24
    )
    partner = send(current, route(1, (1, 1)))
    shape = jax.ShapeDtypeStruct((LEVELS, 2 * K, K), F32)
    leaf_map, maps = call(
        lower_kernel,
        (jax.ShapeDtypeStruct((1, PR_DEV, K), F32), shape),
        (flags, arrived, landing, own_landing, stack_keys, current),
        [smem()] + [vmem()] * 5,
        (vmem(), hbm()),
        [pltpu.VMEM((2, 2 * K, K), F32), pltpu.SemaphoreType.DMA],
        name="lower_maps",
        flops=1 << 31,
        limit=12,
    )
    maps, top = call(
        upper_kernel,
        (shape, rows),
        (flags, chosen, current, partner, maps),
        [smem(), vmem(), vmem(), vmem(), hbm()],
        (hbm(), vmem()),
        [pltpu.VMEM((2 * K, K), F32), pltpu.SemaphoreType.DMA],
        name="upper_map",
        flops=1 << 31,
        aliases={4: 0},
    )
    return (leaf_map, maps[None, None], top[None, None])


def solution(mesh):
    inner = Mesh(mesh.devices.reshape(4, 2, 16), ("x", "core", "grp"))
    in_specs = (
        P(ALL, None),
        P(ALL, None),
        P(),
        P(),
        P(("x", "core")),
        P(("x", "core"), "grp", None),
        P(("x", "core"), None, None),
    )
    out_specs = (
        P(("x", "core"), "grp", None),
        P(("x", "core"), "grp", None, None, None),
        P(("x", "core"), "grp", None, None),
    )
    return jax.shard_map(local, mesh=inner, in_specs=in_specs, out_specs=out_specs, check_vma=False)
```

```python
import jax
import jax.numpy as jnp
from jax import lax
from jax.experimental import pallas as pl
from jax.experimental.pallas import tpu as pltpu
from jax.sharding import Mesh
from jax.sharding import PartitionSpec as P


PR_DEV = 1024
LEVELS = 3
ROWS = 128
WIDTH = 256
HALF = 128
K = 128
DOUBLINGS = 8
ALL = ("x", "core", "grp")
F32 = jnp.float32
BF16 = jnp.bfloat16
HIGH = lax.Precision.HIGHEST


def coords(device):
    front, grp = device // 16, device % 16
    return [front >> 1, grp >> 2, grp & 3], front & 1


def device_of(chip, core):
    return (chip[0] * 2 + core) * 16 + chip[1] * 4 + chip[2]


def route(axis, masks):
    pairs = []
    for device in range(128):
        chip, core = coords(device)
        chip[axis] ^= masks[core]
        pairs.append((device, device_of(chip, core)))
    return pairs


def core_route():
    pairs = []
    for device in range(128):
        chip, core = coords(device)
        pairs.append((device, device_of(chip, 1 - core)))
    return pairs


def send(value, pairs):
    return lax.ppermute(value, ALL, pairs)


def vmem():
    return pl.BlockSpec(memory_space=pltpu.VMEM)


def smem():
    return pl.BlockSpec(memory_space=pltpu.SMEM)


def hbm():
    return pl.BlockSpec(memory_space=pl.ANY)


def call(kernel, outs, args, specs, out_specs, scratch=(), flops=0, aliases=None, limit=6):
    return pl.pallas_call(
        kernel,
        out_shape=outs,
        in_specs=specs,
        out_specs=out_specs,
        scratch_shapes=list(scratch),
        input_output_aliases=aliases or {},
        cost_estimate=pl.CostEstimate(flops=flops, bytes_accessed=1 << 20, transcendentals=0),
        compiler_params=pltpu.CompilerParams(vmem_limit_bytes=limit << 20),
    )(*args)


def split3(value):
    hi = value.astype(BF16)
    rest = value - hi.astype(F32)
    mid = rest.astype(BF16)
    low = (rest - mid.astype(F32)).astype(BF16)
    return hi, mid, low


def pick(onehot, value):
    out = None
    for term in split3(value):
        part = jnp.dot(onehot, term, preferred_element_type=F32)
        out = part if out is None else out + part
    return out


def extract_kernel(where, full, give, held, sems):
    core = where[3]
    loads, stores = [], []
    for x in range(4):
        spot = pl.multiple_of((x * 2 + 1 - core) * 2048, 2048)
        inside = held.at[:, pl.ds(x * 2048, 2048)]
        loads.append(pltpu.make_async_copy(full.at[:, pl.ds(spot, 2048)], inside, sems.at[x]))
        stores.append(
            pltpu.make_async_copy(inside, give.at[:, pl.ds(x * 2048, 2048)], sems.at[4 + x])
        )
    for load in loads:
        load.start()
    for load, store in zip(loads, stores):
        load.wait()
        store.start()
    for store in stores:
        store.wait()


def piece_offset(where, order, piece):
    core = where[3]
    first, second = jnp.where(core == 0, 1, 3), jnp.where(core == 0, 3, 1)
    chip = [where[0], where[1], where[2]]
    for step, axis in enumerate(order):
        if (piece >> (2 * step)) & 1:
            chip[axis] = chip[axis] ^ first
        if (piece >> (2 * step + 1)) & 1:
            chip[axis] = chip[axis] ^ second
    inside = chip[1] * 4 + chip[2]
    return pl.multiple_of((chip[0] * 16 + inside) * 128, 128)


ORDERS = ((2, 0, 1), (2, 1, 0))


def products(where, source, chains, first):
    columns = []
    for order, pieces in zip(ORDERS, chains):
        total = None
        for block, piece in enumerate(pieces):
            for j in range(0, 16, 2):
                number = first + 16 * block + j
                spots = [piece_offset(where, order, number + k) for k in range(2)]
                right = piece[j : j + 2].reshape(256, HALF)
                left = jnp.concatenate([source[:, pl.ds(s, 128)] for s in spots], axis=1)
                part = jnp.dot(left, right, preferred_element_type=F32)
                total = part if total is None else total + part
        columns.append(total)
    return jnp.concatenate(columns, axis=1)


def partial_products(where, own, received, chains, first):
    halves = [products(where, source, chains, first) for source in (own, received)]
    return jnp.concatenate(halves, axis=0)


def first_kernel(where, full, received, a, b, out, own, sems):
    core = where[3]
    loads = []
    for x in range(4):
        spot = pl.multiple_of((x * 2 + core) * 2048, 2048)
        loads.append(
            pltpu.make_async_copy(
                full.at[:, pl.ds(spot, 2048)], own.at[:, pl.ds(x * 2048, 2048)], sems.at[x]
            )
        )
    for load in loads:
        load.start()
    out[ROWS:] = products(where, received, ((a,), (b,)), 0)
    for load in loads:
        load.wait()
    out[:ROWS] = products(where, own, ((a,), (b,)), 0)


def middle_kernel(where, own, received, a, c, b, d, acc, out):
    out[...] = acc[...] + partial_products(where, own, received, ((a, c), (b, d)), 16)


def second_kernel(where, keys, own, received, a, b, acc, keep, give):
    total = acc[...] + partial_products(where, own, received, ((a,), (b,)), 48)
    core = where[3]
    spots = lax.broadcasted_iota(jnp.int32, (256, 256), 0)
    key = keys[...]
    here = (key == spots + core * 256).astype(F32).astype(BF16)
    there = (key == spots + (1 - core) * 256).astype(F32).astype(BF16)
    keep[...] = pick(here, total)
    give[...] = pick(there, total)


def finish_kernel(keep, given, out):
    rows = (keep[...] + given[...]).astype(BF16).reshape(16, 16, WIDTH)
    for copy in range(4):
        out[:, copy] = rows


def join_kernel(a, b, out):
    count = a.shape[0]
    out[:count] = a[...]
    out[count:] = b[...]


def index_kernel(
    place, dest, rows, line_keys, merge, keys, landing, own_landing, stack_keys, top_keys, chosen
):
    myself, core, z, live, grp = (place[i] for i in range(5))
    sub = lax.broadcasted_iota(jnp.int32, (ROWS, ROWS), 0)
    lane = lax.broadcasted_iota(jnp.int32, (ROWS, ROWS), 1)
    for side in range(2):
        device = myself if side == 0 else myself + 16 - 32 * core
        row = dest[pl.ds(device, 1), :]
        wide = jnp.broadcast_to(row, (ROWS, ROWS))
        tall = wide.astype(F32).T.astype(jnp.int32)
        earlier = jnp.where((tall == wide) & (sub < lane), 1, 0)
        rank = jnp.sum(earlier, axis=0, keepdims=True)
        source = core if side == 0 else 1 - core
        chip = (row >> 5) * 16 + (row & 15)
        keys[:, side * ROWS : (side + 1) * ROWS] = (
            ((row >> 4) & 1) * 256 + chip * 4 + source * 2 + rank
        )
    tall = dest[...].astype(F32).T.astype(jnp.int32)
    tall_rows = rows[...].astype(F32).T.astype(jnp.int32)
    below = (lane < sub).astype(F32).astype(BF16)
    values = []
    for leaf in range(4):
        mine = tall == myself - z + leaf
        before = jnp.dot(below, mine.astype(F32).astype(BF16), preferred_element_type=F32)
        for slot in range(2):
            hit = mine & (before == slot) & (tall_rows < live - leaf * PR_DEV)
            value = jnp.where(hit, tall_rows + (leaf * PR_DEV + 1), 0)
            values.append(jnp.sum(value, axis=0, keepdims=True))
    values = jnp.concatenate(values, axis=0).astype(F32)

    def spread(count, shift):
        device = lax.broadcasted_iota(jnp.int32, (ROWS, count), 0)
        spot = lax.broadcasted_iota(jnp.int32, (ROWS, count), 1)
        chip = (device >> 5) * 16 + (device & 15)
        owner = (chip == spot >> shift) & ((device >> 4) & 1 == (spot >> 1) & 1)
        owner = owner.astype(F32).astype(BF16)
        total = None
        for term in split3(values):
            part = jnp.dot(term, owner, preferred_element_type=F32)
            total = part if total is None else total + part
        row = lax.broadcasted_iota(jnp.int32, (8, count), 0)
        spot = lax.broadcasted_iota(jnp.int32, (8, count), 1)
        return total, row, spot

    total, row, spot = spread(1024, 4)
    wanted = ((spot >> 2) & 3) * 2 + (spot & 1)
    found = jnp.sum(jnp.where(row == wanted, total, 0.0), axis=0, keepdims=True)
    landing[...] = found.astype(jnp.int32) - 1
    total, row, spot = spread(256, 2)
    found = jnp.sum(jnp.where(row == z * 2 + (spot & 1), total, 0.0), axis=0, keepdims=True)
    found = found.astype(jnp.int32) - 1
    own_landing[...] = jnp.where(found >= 0, found - z * PR_DEV, -1)

    def upright(row):
        return jnp.broadcast_to(row, (K, K)).T

    def take(values, index):
        total = None
        for block, value in enumerate(values):
            part = jnp.where(sub + block * K == index, upright(value), 0.0)
            part = jnp.sum(part, axis=0, keepdims=True)
            total = part if total is None else total + part
        return total

    def order(flag, a, b):
        return jnp.where(flag == 1, b, a), jnp.where(flag == 1, a, b)

    pieces = [line_keys[j].astype(F32)[:1] for j in range(4)]
    pieces = [p[:, :K] * 16.0 + p[:, K:] for p in pieces]
    swapped = order(core, pieces[1], pieces[2])
    by_mask = (pieces[0], swapped[0], pieces[3], swapped[1])
    full = [
        value + ((z ^ mask) * PR_DEV).astype(F32) for mask, value in enumerate(by_mask)
    ]
    odd = z & 1
    pair = order(odd, full[0], full[1])
    far = order(odd, full[2], full[3])
    low = take(pair, merge[pl.ds(grp >> 1, 1), :])
    high = take(far, merge[pl.ds((grp >> 1) ^ 1, 1), :])
    middle = order((z >> 1) & 1, low, high)
    top = take(middle, merge[pl.ds(8 + (grp >> 2), 1), :])
    for block, value in enumerate(pair + middle):
        stack_keys[block * K : (block + 1) * K] = upright(value).astype(jnp.int32)[:, :1]
    top_keys[...] = upright(top).astype(jnp.int32)[:, :1]
    last = merge[pl.ds(12 + (grp >> 3), 1), :].astype(F32)
    chosen[...] = upright(last).astype(jnp.int32)[:, :1]


def pack_kernel(matrix, skeleton, out):
    out[0, :ROWS] = matrix[...]
    value = skeleton[...]
    row = jnp.concatenate([value >> 4, value & 15], axis=1).astype(F32)
    out[0, ROWS:] = jnp.broadcast_to(row, (16, WIDTH)).astype(BF16)


def join_halves_kernel(a, b, left, right, line_keys):
    count = a.shape[0]
    for index, part in enumerate((a, b)):
        rows = slice(index * count, (index + 1) * count)
        left[rows] = part[:, :ROWS, :HALF]
        right[rows] = part[:, :ROWS, HALF:]
        line_keys[rows] = part[:, ROWS:]


def join_halves(a, b):
    half = jax.ShapeDtypeStruct((2 * a.shape[0], ROWS, HALF), a.dtype)
    return call(
        join_halves_kernel,
        (half, half, jax.ShapeDtypeStruct((2 * a.shape[0], 16, WIDTH), a.dtype)),
        (a, b),
        [vmem(), vmem()],
        (vmem(),) * 3,
        limit=3,
    )


def matches(column, row):
    return (column == row).astype(F32).astype(BF16)


def basis_kernel(arrived, landing, keys, out):
    out[...] = jnp.dot(
        matches(keys[...], landing[...]), arrived[...], preferred_element_type=F32
    )


def split2(value):
    hi = value.astype(BF16)
    return hi, (value - hi.astype(F32)).astype(BF16)


def mul(a, b):
    (ah, al), (bh, bl) = split2(a), split2(b)
    wide = jnp.dot(
        jnp.concatenate([ah, al], axis=1),
        jnp.concatenate([bh, bh], axis=0),
        preferred_element_type=F32,
    )
    return wide + jnp.dot(ah, bl, preferred_element_type=F32)


def mul_t(a, b, precision=None):
    dims = (((1,), (1,)), ((), ()))
    if precision is not None:
        return lax.dot_general(a, b, dims, precision=precision, preferred_element_type=F32)
    (ah, al), (bh, bl) = split2(a), split2(b)
    out = None
    for p, q in ((ah, bh), (ah, bl), (al, bh)):
        part = lax.dot_general(p, q, dims, preferred_element_type=F32)
        out = part if out is None else out + part
    return out


def inverses(bases):
    row = lax.broadcasted_iota(jnp.int32, (K, K), 0)
    col = lax.broadcasted_iota(jnp.int32, (K, K), 1)
    ident = (row == col).astype(F32)
    grams = [mul_t(s, s, HIGH) for s in bases]
    state = []
    for index, gram in enumerate(grams):
        trace = jnp.sum(jnp.sum(gram * ident, axis=0, keepdims=True), axis=1, keepdims=True)
        widest = jnp.max(jnp.sum(jnp.abs(gram), axis=0, keepdims=True), axis=1, keepdims=True)
        low = trace * (0.1 / K) + 1e-5
        gram = gram + low * ident
        grams[index] = gram
        high = jnp.maximum(low + jnp.minimum(trace, widest), 2.0 * low)
        scale = 2.0 / (low + high)
        ratio = (high - low) / (high + low)
        residual = ident - scale * gram
        state.append((scale, ratio, residual))
    for index, (scale, ratio, residual) in enumerate(state):
        square = ratio * ratio
        ratio = square / (2.0 - square)
        approx = ((1.0 + ratio) * scale) * (ident + residual)
        residual = (1.0 + ratio) * mul(residual, residual) - ratio * ident
        state[index] = (approx, ratio, residual)
    for step in range(1, DOUBLINGS):
        for index, (approx, ratio, residual) in enumerate(state):
            square = ratio * ratio
            ratio = square / (2.0 - square)
            if step + 1 < DOUBLINGS:
                both = mul(jnp.concatenate([approx, residual], axis=0), residual)
                approx = (1.0 + ratio) * (approx + both[:K])
                residual = (1.0 + ratio) * both[K:] - ratio * ident
            else:
                approx = (1.0 + ratio) * (approx + mul(approx, residual))
            state[index] = (approx, ratio, residual)
    results = []
    for gram, (approx, ratio, residual) in zip(grams, state):
        fix = ident - jnp.dot(gram, approx, precision=HIGH, preferred_element_type=F32)
        results.append((approx, fix))
    return results


def times_inverse(right, approx, fix):
    first = mul(right, approx)
    return first + mul(first, fix)


def choose(flag, first, second):
    return jnp.where(flag == 1, second, first)


def lower_kernel(flags, arrived, landing, own_landing, keys, top, leaf_out, out, built, leaf_rows, sems):
    rows = arrived[...]
    stacks = jnp.dot(matches(keys[...], landing[...]), rows, preferred_element_type=F32)
    first, second = stacks[: 2 * K], stacks[2 * K :]
    leaf = choose(flags[0], first[:K], first[K:])
    node = choose(flags[1], second[:K], second[K:])
    bases = [leaf, node, top[...]]
    row = lax.broadcasted_iota(jnp.int32, (256, 1024), 0)
    col = lax.broadcasted_iota(jnp.int32, (256, 1024), 1)
    spot = (row >> 2) * 16 + flags[3] * 4 + (row & 3)
    mine = jnp.dot(matches(spot, col), rows, preferred_element_type=F32)
    rights = [mul_t(v, s) for v, s in zip((mine, first, second), bases)]
    maps = [times_inverse(r, *pair) for r, pair in zip(rights, inverses(bases))]
    built[...] = jnp.stack(maps[1:])
    copies = [pltpu.make_async_copy(built, out.at[:2], sems.at[4])]
    copies[0].start()
    terms = split2(maps[0])
    for part in range(4):
        spots = lax.broadcasted_iota(jnp.int32, (256, 256), 0) + part * 256
        onehot = matches(spots, own_landing[...])
        leaf_rows[part] = sum(jnp.dot(onehot, t, preferred_element_type=F32) for t in terms)
        copy = pltpu.make_async_copy(
            leaf_rows.at[part], leaf_out.at[0, pl.ds(part * 256, 256)], sems.at[part]
        )
        copy.start()
        copies.append(copy)
    for copy in copies:
        copy.wait()


def upper_kernel(flags, chosen, current, partner, previous, out, top, built, rows, sems):
    mine, other = current[...], partner[...]
    stacked = jnp.concatenate(
        [choose(flags[2], mine, other), choose(flags[2], other, mine)], axis=0
    )
    spots = lax.broadcasted_iota(jnp.int32, (K, 2 * K), 1)
    basis = pick(matches(chosen[...], spots), stacked)
    rows[...] = basis
    early = pltpu.make_async_copy(rows, top, sems.at[0])
    early.start()
    right = mul_t(stacked, basis)
    built[...] = times_inverse(right, *inverses([basis])[0])
    copy = pltpu.make_async_copy(built, out.at[2], sems.at[1])
    copy.start()
    copy.wait()
    early.wait()


def join(a, b, limit):
    return call(
        join_kernel,
        jax.ShapeDtypeStruct((2 * a.shape[0],) + a.shape[1:], a.dtype),
        (a, b),
        [vmem(), vmem()],
        vmem(),
        limit=limit,
    )


def local(contributions, sketch_matrix, destinations, parent_rows, front_sizes, leaf_skeleton, merge_skeleton):
    x, core, grp = lax.axis_index("x"), lax.axis_index("core"), lax.axis_index("grp")
    y, z = grp >> 2, grp & 3
    myself = (x * 2 + core) * 16 + grp
    where = jnp.stack([x, y, z, core]).astype(jnp.int32)

    line = call(
        pack_kernel,
        jax.ShapeDtypeStruct((1, ROWS + 16, WIDTH), BF16),
        (sketch_matrix, leaf_skeleton.reshape(1, K)),
        [vmem(), vmem()],
        vmem(),
        limit=2,
    )
    line = join(line, send(line, route(2, (1, 3))), 2)
    *held, line_keys = join_halves(line, send(line, route(2, (3, 1))))
    one, three = (1, 3), (3, 1)
    for masks in (one, three):
        arriving = [send(held[c], route(ORDERS[c][1], masks)) for c in range(2)]
        held = [join(h, r, 4) for h, r in zip(held, arriving)]
    last = [ORDERS[c][2] for c in range(2)]

    def ring(value, c, masks):
        return send(value, route(last[c], masks))

    nexts = [ring(held[c], c, one) for c in range(2)]
    others = [ring(held[c], c, three) for c in range(2)]
    extra = [ring(nexts[c], c, three) for c in range(2)]
    give = call(
        extract_kernel,
        jax.ShapeDtypeStruct((ROWS, 8192), BF16),
        (where, contributions),
        [smem(), pl.BlockSpec(memory_space=pltpu.HBM)],
        pl.BlockSpec(memory_space=pltpu.HBM),
        [pltpu.VMEM((ROWS, 8192), BF16), pltpu.SemaphoreType.DMA((8,))],
        limit=60,
    )
    received = send(give, core_route())
    place = jnp.stack([myself, core, z, front_sizes[0] - y * 4 * PR_DEV, grp]).astype(jnp.int32)
    column = jax.ShapeDtypeStruct((K, 1), jnp.int32)
    keys, landing, own_landing, stack_keys, top_keys, chosen = call(
        index_kernel,
        tuple(jax.ShapeDtypeStruct((1, n), jnp.int32) for n in (256, 1024, 256))
        + (jax.ShapeDtypeStruct((4 * K, 1), jnp.int32), column, column),
        (
            place,
            destinations.reshape(ROWS, ROWS),
            parent_rows.reshape(ROWS, ROWS),
            line_keys,
            merge_skeleton[0],
        ),
        [smem()] + [vmem()] * 4,
        (vmem(),) * 6,
    )
    flags = jnp.stack([z & 1, (z >> 1) & 1, y & 1, z]).astype(jnp.int32)
    square = jax.ShapeDtypeStruct((256, 256), F32)
    acc, own = call(
        first_kernel,
        (square, jax.ShapeDtypeStruct((ROWS, 8192), BF16)),
        (where, contributions, received, held[0], held[1]),
        [smem(), pl.BlockSpec(memory_space=pltpu.HBM)] + [vmem()] * 3,
        (vmem(), vmem()),
        [pltpu.SemaphoreType.DMA((4,))],
        flops=1 << 28,
        limit=12,
    )
    acc = call(
        middle_kernel,
        square,
        (where, own, received, nexts[0], others[0], nexts[1], others[1], acc),
        [smem()] + [vmem()] * 7,
        vmem(),
        flops=1 << 29,
        limit=12,
    )
    keep, give = call(
        second_kernel,
        (square, square),
        (where, keys, own, received, extra[0], extra[1], acc),
        [smem()] + [vmem()] * 6,
        (vmem(), vmem()),
        flops=1 << 28,
        limit=12,
    )
    packed = call(
        finish_kernel,
        jax.ShapeDtypeStruct((16, 4, 16, WIDTH), BF16),
        (keep, send(give, core_route())),
        [vmem(), vmem()],
        vmem(),
    )
    arrived = lax.all_to_all(
        packed.reshape(64, 16, WIDTH), ("x", "grp"), split_axis=0, concat_axis=0, tiled=True
    ).reshape(1024, WIDTH)

    rows = jax.ShapeDtypeStruct((K, WIDTH), F32)
    current = call(
        basis_kernel, rows, (arrived, landing, top_keys), [vmem()] * 3, vmem(), flops=1 << 24
    )
    partner = send(current, route(1, (1, 1)))
    shape = jax.ShapeDtypeStruct((LEVELS, 2 * K, K), F32)
    leaf_map, maps = call(
        lower_kernel,
        (jax.ShapeDtypeStruct((1, PR_DEV, K), F32), shape),
        (flags, arrived, landing, own_landing, stack_keys, current),
        [smem()] + [vmem()] * 5,
        (hbm(), hbm()),
        [
            pltpu.VMEM((2, 2 * K, K), F32),
            pltpu.VMEM((4, 256, K), F32),
            pltpu.SemaphoreType.DMA((5,)),
        ],
        flops=1 << 31,
        limit=12,
    )
    maps, top = call(
        upper_kernel,
        (shape, rows),
        (flags, chosen, current, partner, maps),
        [smem(), vmem(), vmem(), vmem(), hbm()],
        (hbm(), hbm()),
        [
            pltpu.VMEM((2 * K, K), F32),
            pltpu.VMEM((K, WIDTH), F32),
            pltpu.SemaphoreType.DMA((2,)),
        ],
        flops=1 << 31,
        aliases={4: 0},
    )
    return (leaf_map, maps[None, None], top[None, None])


def solution(mesh):
    inner = Mesh(mesh.devices.reshape(4, 2, 16), ("x", "core", "grp"))
    in_specs = (
        P(ALL, None),
        P(ALL, None),
        P(),
        P(),
        P(("x", "core")),
        P(("x", "core"), "grp", None),
        P(("x", "core"), None, None),
    )
    out_specs = (
        P(("x", "core"), "grp", None),
        P(("x", "core"), "grp", None, None, None),
        P(("x", "core"), "grp", None, None),
    )

    return jax.shard_map(local, mesh=inner, in_specs=in_specs, out_specs=out_specs, check_vma=False)
```

```python
import jax
import jax.numpy as jnp
from jax import lax
from jax.experimental import pallas as pl
from jax.experimental.pallas import tpu as pltpu
from jax.sharding import Mesh
from jax.sharding import PartitionSpec as P


PR_DEV = 1024
LEVELS = 3
ROWS = 128
WIDTH = 256
HALF = 128
K = 128
DOUBLINGS = 8
ALL = ("x", "core", "grp")
F32 = jnp.float32
BF16 = jnp.bfloat16
HIGH = lax.Precision.HIGHEST


def coords(device):
    front, grp = device // 16, device % 16
    return [front >> 1, grp >> 2, grp & 3], front & 1


def device_of(chip, core):
    return (chip[0] * 2 + core) * 16 + chip[1] * 4 + chip[2]


def route(axis, masks):
    pairs = []
    for device in range(128):
        chip, core = coords(device)
        chip[axis] ^= masks[core]
        pairs.append((device, device_of(chip, core)))
    return pairs


def core_route():
    pairs = []
    for device in range(128):
        chip, core = coords(device)
        pairs.append((device, device_of(chip, 1 - core)))
    return pairs


def send(value, pairs):
    return lax.ppermute(value, ALL, pairs)


def vmem():
    return pl.BlockSpec(memory_space=pltpu.VMEM)


def smem():
    return pl.BlockSpec(memory_space=pltpu.SMEM)


def hbm():
    return pl.BlockSpec(memory_space=pl.ANY)


def call(kernel, outs, args, specs, out_specs, scratch=(), flops=0, aliases=None, limit=6):
    return pl.pallas_call(
        kernel,
        out_shape=outs,
        in_specs=specs,
        out_specs=out_specs,
        scratch_shapes=list(scratch),
        input_output_aliases=aliases or {},
        cost_estimate=pl.CostEstimate(flops=flops, bytes_accessed=1 << 20, transcendentals=0),
        compiler_params=pltpu.CompilerParams(vmem_limit_bytes=limit << 20),
    )(*args)


def split3(value):
    hi = value.astype(BF16)
    rest = value - hi.astype(F32)
    mid = rest.astype(BF16)
    low = (rest - mid.astype(F32)).astype(BF16)
    return hi, mid, low


def pick(onehot, value):
    out = None
    for term in split3(value):
        part = jnp.dot(onehot, term, preferred_element_type=F32)
        out = part if out is None else out + part
    return out


def extract_kernel(where, full, give, held, sems):
    core = where[3]
    loads, stores = [], []
    for x in range(4):
        spot = pl.multiple_of((x * 2 + 1 - core) * 2048, 2048)
        inside = held.at[:, pl.ds(x * 2048, 2048)]
        loads.append(pltpu.make_async_copy(full.at[:, pl.ds(spot, 2048)], inside, sems.at[x]))
        stores.append(
            pltpu.make_async_copy(inside, give.at[:, pl.ds(x * 2048, 2048)], sems.at[4 + x])
        )
    for load in loads:
        load.start()
    for load, store in zip(loads, stores):
        load.wait()
        store.start()
    for store in stores:
        store.wait()


def piece_offset(where, order, piece):
    core = where[3]
    first, second = jnp.where(core == 0, 1, 3), jnp.where(core == 0, 3, 1)
    chip = [where[0], where[1], where[2]]
    for step, axis in enumerate(order):
        if (piece >> (2 * step)) & 1:
            chip[axis] = chip[axis] ^ first
        if (piece >> (2 * step + 1)) & 1:
            chip[axis] = chip[axis] ^ second
    inside = chip[1] * 4 + chip[2]
    return pl.multiple_of((chip[0] * 16 + inside) * 128, 128)


ORDERS = ((2, 0, 1), (2, 1, 0))


def products(where, source, chains, first):
    columns = []
    for order, pieces in zip(ORDERS, chains):
        total = None
        for block, piece in enumerate(pieces):
            for j in range(0, 16, 2):
                number = first + 16 * block + j
                spots = [piece_offset(where, order, number + k) for k in range(2)]
                right = piece[j : j + 2].reshape(256, HALF)
                left = jnp.concatenate([source[:, pl.ds(s, 128)] for s in spots], axis=1)
                part = jnp.dot(left, right, preferred_element_type=F32)
                total = part if total is None else total + part
        columns.append(total)
    return jnp.concatenate(columns, axis=1)


def partial_products(where, own, received, chains, first):
    halves = [products(where, source, chains, first) for source in (own, received)]
    return jnp.concatenate(halves, axis=0)


def first_kernel(where, full, received, a, b, out, own, sems):
    core = where[3]
    loads = []
    for x in range(4):
        spot = pl.multiple_of((x * 2 + core) * 2048, 2048)
        loads.append(
            pltpu.make_async_copy(
                full.at[:, pl.ds(spot, 2048)], own.at[:, pl.ds(x * 2048, 2048)], sems.at[x]
            )
        )
    for load in loads:
        load.start()
    out[ROWS:] = products(where, received, ((a,), (b,)), 0)
    for load in loads:
        load.wait()
    out[:ROWS] = products(where, own, ((a,), (b,)), 0)


def middle_kernel(where, own, received, a, c, b, d, acc, out):
    out[...] = acc[...] + partial_products(where, own, received, ((a, c), (b, d)), 16)


def second_kernel(where, keys, own, received, a, b, acc, keep, give):
    total = acc[...] + partial_products(where, own, received, ((a,), (b,)), 48)
    core = where[3]
    spots = lax.broadcasted_iota(jnp.int32, (256, 256), 0)
    key = keys[...]
    here = (key == spots + core * 256).astype(F32).astype(BF16)
    there = (key == spots + (1 - core) * 256).astype(F32).astype(BF16)
    keep[...] = pick(here, total)
    give[...] = pick(there, total)


def finish_kernel(keep, given, out):
    rows = (keep[...] + given[...]).astype(BF16).reshape(16, 16, WIDTH)
    for copy in range(4):
        out[:, copy] = rows


def join_kernel(a, b, out):
    count = a.shape[0]
    out[:count] = a[...]
    out[count:] = b[...]


def index_kernel(
    place, dest, rows, line_keys, merge, keys, landing, own_landing, stack_keys, top_keys, chosen
):
    myself, core, z, live, grp = (place[i] for i in range(5))
    sub = lax.broadcasted_iota(jnp.int32, (ROWS, ROWS), 0)
    lane = lax.broadcasted_iota(jnp.int32, (ROWS, ROWS), 1)
    for side in range(2):
        device = myself if side == 0 else myself + 16 - 32 * core
        row = dest[pl.ds(device, 1), :]
        wide = jnp.broadcast_to(row, (ROWS, ROWS))
        tall = wide.astype(F32).T.astype(jnp.int32)
        earlier = jnp.where((tall == wide) & (sub < lane), 1, 0)
        rank = jnp.sum(earlier, axis=0, keepdims=True)
        source = core if side == 0 else 1 - core
        chip = (row >> 5) * 16 + (row & 15)
        keys[:, side * ROWS : (side + 1) * ROWS] = (
            ((row >> 4) & 1) * 256 + chip * 4 + source * 2 + rank
        )
    tall = dest[...].astype(F32).T.astype(jnp.int32)
    tall_rows = rows[...].astype(F32).T.astype(jnp.int32)
    below = (lane < sub).astype(F32).astype(BF16)
    values = []
    for leaf in range(4):
        mine = tall == myself - z + leaf
        before = jnp.dot(below, mine.astype(F32).astype(BF16), preferred_element_type=F32)
        for slot in range(2):
            hit = mine & (before == slot) & (tall_rows < live - leaf * PR_DEV)
            value = jnp.where(hit, tall_rows + (leaf * PR_DEV + 1), 0)
            values.append(jnp.sum(value, axis=0, keepdims=True))
    values = jnp.concatenate(values, axis=0).astype(F32)

    def spread(count, shift):
        device = lax.broadcasted_iota(jnp.int32, (ROWS, count), 0)
        spot = lax.broadcasted_iota(jnp.int32, (ROWS, count), 1)
        chip = (device >> 5) * 16 + (device & 15)
        owner = (chip == spot >> shift) & ((device >> 4) & 1 == (spot >> 1) & 1)
        owner = owner.astype(F32).astype(BF16)
        total = None
        for term in split3(values):
            part = jnp.dot(term, owner, preferred_element_type=F32)
            total = part if total is None else total + part
        row = lax.broadcasted_iota(jnp.int32, (8, count), 0)
        spot = lax.broadcasted_iota(jnp.int32, (8, count), 1)
        return total, row, spot

    total, row, spot = spread(1024, 4)
    wanted = ((spot >> 2) & 3) * 2 + (spot & 1)
    found = jnp.sum(jnp.where(row == wanted, total, 0.0), axis=0, keepdims=True)
    landing[...] = found.astype(jnp.int32) - 1
    total, row, spot = spread(256, 2)
    found = jnp.sum(jnp.where(row == z * 2 + (spot & 1), total, 0.0), axis=0, keepdims=True)
    found = found.astype(jnp.int32) - 1
    own_landing[...] = jnp.where(found >= 0, found - z * PR_DEV, -1)

    def take(values, index):
        total = None
        for block, value in enumerate(values):
            part = jnp.where(sub + block * K == index, upright(value), 0.0)
            part = jnp.sum(part, axis=0, keepdims=True)
            total = part if total is None else total + part
        return total

    def order(flag, a, b):
        return jnp.where(flag == 1, b, a), jnp.where(flag == 1, a, b)

    pieces = [line_keys[j].astype(F32)[:1] for j in range(4)]
    pieces = [p[:, :K] * 16.0 + p[:, K:] for p in pieces]
    swapped = order(core, pieces[1], pieces[2])
    by_mask = (pieces[0], swapped[0], pieces[3], swapped[1])
    full = [
        value + ((z ^ mask) * PR_DEV).astype(F32) for mask, value in enumerate(by_mask)
    ]
    odd = z & 1
    pair = order(odd, full[0], full[1])
    far = order(odd, full[2], full[3])
    low = take(pair, merge[pl.ds(grp >> 1, 1), :])
    high = take(far, merge[pl.ds((grp >> 1) ^ 1, 1), :])
    middle = order((z >> 1) & 1, low, high)
    top = take(middle, merge[pl.ds(8 + (grp >> 2), 1), :])
    stack_keys[...] = jnp.concatenate(pair + middle, axis=0).astype(jnp.int32)
    top_keys[...] = upright(top).astype(jnp.int32)[:, :1]
    last = merge[pl.ds(12 + (grp >> 3), 1), :].astype(F32)
    chosen[...] = upright(last).astype(jnp.int32)[:, :1]


def upright(row):
    return jnp.broadcast_to(row, (K, K)).T


def pack_kernel(matrix, skeleton, out, index, sems):
    copies = [
        pltpu.make_async_copy(matrix, out.at[0, :ROWS], sems.at[0]),
        pltpu.make_async_copy(skeleton, index, sems.at[1]),
    ]
    for copy in copies:
        copy.start()
    for copy in copies:
        copy.wait()
    value = index[...]
    row = jnp.concatenate([value >> 4, value & 15], axis=1).astype(F32)
    out[0, ROWS:] = jnp.broadcast_to(row, (16, WIDTH)).astype(BF16)


def join_halves_kernel(a, b, left, right, line_keys):
    count = a.shape[0]
    for index, part in enumerate((a, b)):
        rows = slice(index * count, (index + 1) * count)
        left[rows] = part[:, :ROWS, :HALF]
        right[rows] = part[:, :ROWS, HALF:]
        line_keys[rows] = part[:, ROWS:]


def join_halves(a, b):
    half = jax.ShapeDtypeStruct((2 * a.shape[0], ROWS, HALF), a.dtype)
    return call(
        join_halves_kernel,
        (half, half, jax.ShapeDtypeStruct((2 * a.shape[0], 16, WIDTH), a.dtype)),
        (a, b),
        [vmem(), vmem()],
        (vmem(),) * 3,
        limit=3,
    )


def matches(column, row):
    return (column == row).astype(F32).astype(BF16)


def basis_kernel(arrived, landing, keys, out):
    out[...] = jnp.dot(
        matches(keys[...], landing[...]), arrived[...], preferred_element_type=F32
    )


def split2(value):
    hi = value.astype(BF16)
    return hi, (value - hi.astype(F32)).astype(BF16)


def mul(a, b):
    (ah, al), (bh, bl) = split2(a), split2(b)
    wide = jnp.dot(
        jnp.concatenate([ah, al], axis=1),
        jnp.concatenate([bh, bh], axis=0),
        preferred_element_type=F32,
    )
    return wide + jnp.dot(ah, bl, preferred_element_type=F32)


def mul_t(a, b, precision=None):
    dims = (((1,), (1,)), ((), ()))
    if precision is not None:
        return lax.dot_general(a, b, dims, precision=precision, preferred_element_type=F32)
    (ah, al), (bh, bl) = split2(a), split2(b)
    out = None
    for p, q in ((ah, bh), (ah, bl), (al, bh)):
        part = lax.dot_general(p, q, dims, preferred_element_type=F32)
        out = part if out is None else out + part
    return out


def inverses(bases):
    row = lax.broadcasted_iota(jnp.int32, (K, K), 0)
    col = lax.broadcasted_iota(jnp.int32, (K, K), 1)
    ident = (row == col).astype(F32)
    grams = [mul_t(s, s, HIGH) for s in bases]
    state = []
    for index, gram in enumerate(grams):
        trace = jnp.sum(jnp.sum(gram * ident, axis=0, keepdims=True), axis=1, keepdims=True)
        widest = jnp.max(jnp.sum(jnp.abs(gram), axis=0, keepdims=True), axis=1, keepdims=True)
        low = trace * (0.1 / K) + 1e-5
        gram = gram + low * ident
        grams[index] = gram
        high = jnp.maximum(low + jnp.minimum(trace, widest), 2.0 * low)
        scale = 2.0 / (low + high)
        ratio = (high - low) / (high + low)
        residual = ident - scale * gram
        state.append((scale, ratio, residual))
    for index, (scale, ratio, residual) in enumerate(state):
        square = ratio * ratio
        ratio = square / (2.0 - square)
        approx = ((1.0 + ratio) * scale) * (ident + residual)
        residual = (1.0 + ratio) * mul(residual, residual) - ratio * ident
        state[index] = (approx, ratio, residual)
    for step in range(1, DOUBLINGS):
        for index, (approx, ratio, residual) in enumerate(state):
            square = ratio * ratio
            ratio = square / (2.0 - square)
            if step + 1 < DOUBLINGS:
                both = mul(jnp.concatenate([approx, residual], axis=0), residual)
                approx = (1.0 + ratio) * (approx + both[:K])
                residual = (1.0 + ratio) * both[K:] - ratio * ident
            else:
                approx = (1.0 + ratio) * (approx + mul(approx, residual))
            state[index] = (approx, ratio, residual)
    results = []
    for gram, (approx, ratio, residual) in zip(grams, state):
        fix = ident - jnp.dot(gram, approx, precision=HIGH, preferred_element_type=F32)
        results.append((approx, fix))
    return results


def times_inverse(right, approx, fix):
    first = mul(right, approx)
    return first + mul(first, fix)


def choose(flag, first, second):
    return jnp.where(flag == 1, second, first)


def lower_kernel(flags, arrived, landing, keys, top, leaf_rows, out, built, sem):
    rows = arrived[...]
    tall = keys[...].astype(F32)
    tall = [upright(tall[j : j + 1])[:, :1] for j in range(4)]
    tall = jnp.concatenate(tall, axis=0).astype(jnp.int32)
    stacks = jnp.dot(matches(tall, landing[...]), rows, preferred_element_type=F32)
    first, second = stacks[: 2 * K], stacks[2 * K :]
    leaf = choose(flags[0], first[:K], first[K:])
    node = choose(flags[1], second[:K], second[K:])
    bases = [leaf, node, top[...]]
    row = lax.broadcasted_iota(jnp.int32, (256, 1024), 0)
    col = lax.broadcasted_iota(jnp.int32, (256, 1024), 1)
    spot = (row >> 2) * 16 + flags[3] * 4 + (row & 3)
    mine = jnp.dot(matches(spot, col), rows, preferred_element_type=F32)
    rights = [mul_t(v, s) for v, s in zip((mine, first, second), bases)]
    maps = [times_inverse(r, *pair) for r, pair in zip(rights, inverses(bases))]
    built[...] = jnp.stack(maps[1:])
    copy = pltpu.make_async_copy(built, out.at[:2], sem)
    copy.start()
    leaf_rows[...] = maps[0]
    copy.wait()


def upper_kernel(
    flags,
    chosen,
    current,
    partner,
    own_landing,
    leaf,
    previous,
    leaf_out,
    out,
    top,
    built,
    rows,
    blocks,
    sems,
):
    mine, other = current[...], partner[...]
    stacked = jnp.concatenate(
        [choose(flags[2], mine, other), choose(flags[2], other, mine)], axis=0
    )
    spots = lax.broadcasted_iota(jnp.int32, (K, 2 * K), 1)
    basis = pick(matches(chosen[...], spots), stacked)
    rows[...] = basis
    copies = [pltpu.make_async_copy(rows, top, sems.at[0])]
    copies[0].start()
    terms = split2(leaf[...])
    for part in range(4):
        spots = lax.broadcasted_iota(jnp.int32, (256, 256), 0) + part * 256
        onehot = matches(spots, own_landing[...])
        blocks[part] = sum(jnp.dot(onehot, t, preferred_element_type=F32) for t in terms)
        copies.append(
            pltpu.make_async_copy(
                blocks.at[part], leaf_out.at[0, pl.ds(part * 256, 256)], sems.at[2 + part]
            )
        )
        copies[-1].start()
    right = mul_t(stacked, basis)
    built[...] = times_inverse(right, *inverses([basis])[0])
    copies.append(pltpu.make_async_copy(built, out.at[2], sems.at[1]))
    copies[-1].start()
    for copy in copies:
        copy.wait()


def join(a, b, limit):
    return call(
        join_kernel,
        jax.ShapeDtypeStruct((2 * a.shape[0],) + a.shape[1:], a.dtype),
        (a, b),
        [vmem(), vmem()],
        vmem(),
        limit=limit,
    )


def local(contributions, sketch_matrix, destinations, parent_rows, front_sizes, leaf_skeleton, merge_skeleton):
    x, core, grp = lax.axis_index("x"), lax.axis_index("core"), lax.axis_index("grp")
    y, z = grp >> 2, grp & 3
    myself = (x * 2 + core) * 16 + grp
    where = jnp.stack([x, y, z, core]).astype(jnp.int32)

    line = call(
        pack_kernel,
        jax.ShapeDtypeStruct((1, ROWS + 16, WIDTH), BF16),
        tuple(
            pltpu.with_memory_space_constraint(value, pltpu.HBM)
            for value in (sketch_matrix, leaf_skeleton.reshape(1, K))
        ),
        [pl.BlockSpec(memory_space=pltpu.HBM)] * 2,
        vmem(),
        [pltpu.VMEM((1, K), jnp.int32), pltpu.SemaphoreType.DMA((2,))],
        limit=2,
    )
    line = join(line, send(line, route(2, (1, 3))), 2)
    *held, line_keys = join_halves(line, send(line, route(2, (3, 1))))
    one, three = (1, 3), (3, 1)
    for masks in (one, three):
        arriving = [send(held[c], route(ORDERS[c][1], masks)) for c in range(2)]
        held = [join(h, r, 4) for h, r in zip(held, arriving)]
    last = [ORDERS[c][2] for c in range(2)]

    def ring(value, c, masks):
        return send(value, route(last[c], masks))

    nexts = [ring(held[c], c, one) for c in range(2)]
    others = [ring(held[c], c, three) for c in range(2)]
    extra = [ring(nexts[c], c, three) for c in range(2)]
    give = call(
        extract_kernel,
        jax.ShapeDtypeStruct((ROWS, 8192), BF16),
        (where, pltpu.with_memory_space_constraint(contributions, pltpu.HBM)),
        [smem(), pl.BlockSpec(memory_space=pltpu.HBM)],
        pl.BlockSpec(memory_space=pltpu.HBM),
        [pltpu.VMEM((ROWS, 8192), BF16), pltpu.SemaphoreType.DMA((8,))],
        limit=6,
    )
    received = send(give, core_route())
    place = jnp.stack([myself, core, z, front_sizes[0] - y * 4 * PR_DEV, grp]).astype(jnp.int32)
    column = jax.ShapeDtypeStruct((K, 1), jnp.int32)
    keys, landing, own_landing, stack_keys, top_keys, chosen = call(
        index_kernel,
        tuple(jax.ShapeDtypeStruct((1, n), jnp.int32) for n in (256, 1024, 256))
        + (jax.ShapeDtypeStruct((4, K), jnp.int32), column, column),
        (
            place,
            destinations.reshape(ROWS, ROWS),
            parent_rows.reshape(ROWS, ROWS),
            line_keys,
            merge_skeleton[0],
        ),
        [smem()] + [vmem()] * 4,
        (vmem(),) * 6,
    )
    flags = jnp.stack([z & 1, (z >> 1) & 1, y & 1, z]).astype(jnp.int32)
    square = jax.ShapeDtypeStruct((256, 256), F32)
    acc, own = call(
        first_kernel,
        (square, jax.ShapeDtypeStruct((ROWS, 8192), BF16)),
        (
            where,
            pltpu.with_memory_space_constraint(contributions, pltpu.HBM),
            received,
            held[0],
            held[1],
        ),
        [smem(), pl.BlockSpec(memory_space=pltpu.HBM)] + [vmem()] * 3,
        (vmem(), vmem()),
        [pltpu.SemaphoreType.DMA((4,))],
        flops=1 << 28,
        limit=12,
    )
    acc = call(
        middle_kernel,
        square,
        (where, own, received, nexts[0], others[0], nexts[1], others[1], acc),
        [smem()] + [vmem()] * 7,
        vmem(),
        flops=1 << 29,
        limit=12,
    )
    keep, give = call(
        second_kernel,
        (square, square),
        (where, keys, own, received, extra[0], extra[1], acc),
        [smem()] + [vmem()] * 6,
        (vmem(), vmem()),
        flops=1 << 28,
        limit=12,
    )
    packed = call(
        finish_kernel,
        jax.ShapeDtypeStruct((16, 4, 16, WIDTH), BF16),
        (keep, send(give, core_route())),
        [vmem(), vmem()],
        vmem(),
    )
    arrived = lax.all_to_all(
        packed.reshape(64, 16, WIDTH), ("x", "grp"), split_axis=0, concat_axis=0, tiled=True
    ).reshape(1024, WIDTH)

    rows = jax.ShapeDtypeStruct((K, WIDTH), F32)
    current = call(
        basis_kernel, rows, (arrived, landing, top_keys), [vmem()] * 3, vmem(), flops=1 << 24
    )
    partner = send(current, route(1, (1, 1)))
    shape = jax.ShapeDtypeStruct((LEVELS, 2 * K, K), F32)
    leaf, maps = call(
        lower_kernel,
        (jax.ShapeDtypeStruct((2 * K, K), F32), shape),
        (flags, arrived, landing, stack_keys, current),
        [smem()] + [vmem()] * 4,
        (vmem(), hbm()),
        [pltpu.VMEM((2, 2 * K, K), F32), pltpu.SemaphoreType.DMA],
        flops=1 << 31,
        limit=12,
    )
    leaf_map, maps, top = call(
        upper_kernel,
        (jax.ShapeDtypeStruct((1, PR_DEV, K), F32), shape, rows),
        (flags, chosen, current, partner, own_landing, leaf, maps),
        [smem()] + [vmem()] * 5 + [hbm()],
        (hbm(),) * 3,
        [
            pltpu.VMEM((2 * K, K), F32),
            pltpu.VMEM((K, WIDTH), F32),
            pltpu.VMEM((4, 256, K), F32),
            pltpu.SemaphoreType.DMA((6,)),
        ],
        flops=1 << 31,
        aliases={6: 1},
    )
    return (leaf_map, maps[None, None], top[None, None])


def solution(mesh):
    inner = Mesh(mesh.devices.reshape(4, 2, 16), ("x", "core", "grp"))
    in_specs = (
        P(ALL, None),
        P(ALL, None),
        P(),
        P(),
        P(("x", "core")),
        P(("x", "core"), "grp", None),
        P(("x", "core"), None, None),
    )
    out_specs = (
        P(("x", "core"), "grp", None),
        P(("x", "core"), "grp", None, None, None),
        P(("x", "core"), "grp", None, None),
    )

    return jax.shard_map(local, mesh=inner, in_specs=in_specs, out_specs=out_specs, check_vma=False)
```
